32 devices in a mesh: row: 8 (over z, y), col: 4 (over x, core).
Axes of the slice: x: 2, y: 2, z: 4, core: 2. Of those that a mesh axis runs over, the one named last changes fastest.
Arguments:
- tokens: bfloat16 [8192, 2048], P('row', 'col'), may hold values from -6 to 6
- w_query: bfloat16 [2048, 2048], P('row', 'col'), may hold values from -0.125 to 0.125
- w_key: bfloat16 [2048, 1024], P('row', 'col'), may hold values from -0.125 to 0.125
- w_value: bfloat16 [2048, 1024], P('row', 'col'), may hold values from -0.125 to 0.125
- w_out: bfloat16 [2048, 2048], P('row', 'col'), may hold values from -0.75 to 0.75
- w_gate: bfloat16 [2048, 6144], P('row', 'col'), may hold values from -0.125 to 0.125
- w_up: bfloat16 [2048, 6144], P('row', 'col'), may hold values from -0.125 to 0.125
- w_down: bfloat16 [6144, 2048], P('row', 'col'), may hold values from -0.078125 to 0.078125
- attn_gain: float32 [2048], replicated, may hold values from 0.5 to 1.5
- ffn_gain: float32 [2048], replicated, may hold values from 0.5 to 1.5
- query_gain: float32 [128], replicated, may hold values from 0.5 to 1.5
- key_gain: float32 [128], replicated, may hold values from 0.5 to 1.5
- doc_ids: int32 [8, 1024], P('row'), may hold values from 0 to 3, never falling along the last dimension, each value on 1 to 512 neighbouring positions
- out_grad: bfloat16 [8192, 2048], P('row', 'col'), may hold values from -6 to 6
Outputs:
- result: bfloat16 [8192, 2048], P('row', 'col')
- token_grads: float32 [8192, 2048], P('row', 'col')
- query_wgrad: float32 [2048, 2048], P('row', 'col')
- key_wgrad: float32 [2048, 1024], P('row', 'col')
- value_wgrad: float32 [2048, 1024], P('row', 'col')
- out_wgrad: float32 [2048, 2048], P('row', 'col')
- gate_wgrad: float32 [2048, 6144], P('row', 'col')
- up_wgrad: float32 [2048, 6144], P('row', 'col')
- down_wgrad: float32 [6144, 2048], P('row', 'col')
- attn_gain_grad: float32 [2048], replicated
- ffn_gain_grad: float32 [2048], replicated
- query_gain_grad: float32 [128], replicated
- key_gain_grad: float32 [128], replicated
The draws below stay inside these ranges and needn't reach their ends.
Inputs may be any that keep to these rules, and one draw needn't show every extreme that they name: `doc_ids`: numbers documents within each sequence of 1024 tokens, never falling; each document has 1 to 512 tokens and one has exactly that many.
All inputs are finite; a program needn't handle non-finite values.
Results may differ from the reference program's by a relative error of at most 0.018.
Values may be sent and summed in bfloat16 or wider, within the bound.
No kernel may reach another device: no remote copies, remote signals or barrier semaphores. Data moves between devices by JAX's collectives and lax.ppermute only.
A program may use at most 192 MiB of HBM per device.

```python
import math
import jax
import jax.numpy as jnp
import numpy as np
from jax import lax

D = 2048
QH = 16
KVH = 8
HD = 128
FF = 6144
SEQ_LEN = 1024
DOCS = 4
TOKENS = 8192
QW = 2048
KW = 1024
N_ROW = 8


def level_of(own_key, dims, cuts, low, largest):
    gain = 1.0
    for axis_at, parts in cuts:
        steps = jax.random.uniform(jax.random.fold_in(jax.random.fold_in(own_key, 6), axis_at), (parts,), jnp.float32, low / len(cuts), largest / len(cuts))
        gain = gain * jnp.repeat(jnp.exp(steps), dims[axis_at] // parts).reshape((-1,) + (1,) * (len(dims) - 1 - axis_at))
    return gain


def split_up(count, total, bound, lean):
    portions = [(1 << 20) // math.isqrt(standing ** lean) + 1 for standing in range(2, count + 1)]
    spare, given = total - bound - (count - 1), [1] * (count - 1)
    while spare > 0:
        movable = [i for i in range(count - 1) if given[i] < bound]
        pool, budget = sum([portions[i] for i in movable]), spare
        for i in movable:
            extra = min(bound - given[i], max(1, budget * portions[i] // pool), spare)
            given[i] = given[i] + extra
            spare = spare - extra
    return np.array([bound] + given)


def uneven(own_key, number_of, total, limit, skew):
    if number_of == 2:
        one = jax.random.randint(own_key, (), max(1, total - limit), min(limit, total - 1) + 1)
        return jnp.stack([one, total - one])
    sizes = jnp.asarray(split_up(number_of, total, limit, skew), jnp.int32)
    twos = (number_of - 1) // 2
    donor, receiver = sizes[1:1 + 2 * twos:2], sizes[2:2 + 2 * twos:2]
    room = jnp.minimum(donor - 1, limit - receiver)
    shifted = jax.random.randint(jax.random.fold_in(own_key, 1), (twos,), 0, 1 << 20) % (room + 1)
    sizes = sizes.at[1:1 + 2 * twos:2].set(donor - shifted).at[2:2 + 2 * twos:2].set(receiver + shifted)
    return sizes[jax.random.permutation(jax.random.fold_in(own_key, 2), number_of)]


def noise(stream_key, extent, spread, bound, pieces=(), kind=jnp.bfloat16):
    loudness = level_of(stream_key, extent, pieces, -0.22, 0.18) if pieces else 1.0
    values = jax.random.normal(stream_key, extent, jnp.float32) * spread * loudness
    return jnp.minimum(jnp.maximum(values, -bound), bound).astype(kind)


def setup_inputs(seed: int = 0) -> dict:
    streams_of = jax.random.split(jax.random.key(seed), 15)
    tokens = noise(streams_of[0], (TOKENS, D), 1.0, 6.0, ((0, 8), (1, 4)))
    w_query = noise(streams_of[1], (D, QW), D ** -0.5, 0.125, ((0, 8), (1, 4)))
    w_key = noise(streams_of[2], (D, KW), D ** -0.5, 0.125, ((0, 8), (1, 4)))
    w_value = noise(streams_of[3], (D, KW), D ** -0.5, 0.125, ((0, 8), (1, 4)))
    w_out = noise(streams_of[4], (QW, D), (QW // 32) ** -0.5, 0.75, ((0, 8), (1, 4)))
    w_gate = noise(streams_of[5], (D, FF), D ** -0.5, 0.125, ((0, 8), (1, 4)))
    w_up = noise(streams_of[6], (D, FF), D ** -0.5, 0.125, ((0, 8), (1, 4)))
    w_down = noise(streams_of[7], (FF, D), FF ** -0.5, 0.078125, ((0, 8), (1, 4)))
    attn_gain = jnp.clip(1.0 + 0.1 * jax.random.normal(streams_of[8], (D,), jnp.float32), 0.5, 1.5)
    ffn_gain = jnp.clip(1.0 + 0.1 * jax.random.normal(streams_of[9], (D,), jnp.float32), 0.5, 1.5)
    query_gain = jnp.clip(1.0 + 0.1 * jax.random.normal(streams_of[10], (HD,), jnp.float32), 0.5, 1.5)
    key_gain = jnp.clip(1.0 + 0.1 * jax.random.normal(streams_of[11], (HD,), jnp.float32), 0.5, 1.5)
    doc_ids = jax.vmap(lambda own: jnp.searchsorted(jnp.cumsum(uneven(own, DOCS, SEQ_LEN, SEQ_LEN // 2, 2)), jnp.arange(SEQ_LEN), side="right"))(jax.random.split(streams_of[12], N_ROW)).reshape((N_ROW, SEQ_LEN)).astype(jnp.int32)
    out_grad = noise(streams_of[13], (TOKENS, D), 1.0, 6.0, ((0, 8), (1, 4)))
    return dict(tokens=tokens, w_query=w_query, w_key=w_key, w_value=w_value, w_out=w_out, w_gate=w_gate, w_up=w_up, w_down=w_down, attn_gain=attn_gain, ffn_gain=ffn_gain, query_gain=query_gain, key_gain=key_gain, doc_ids=doc_ids, out_grad=out_grad)


EPS = 1e-06
THETA = 1000000.0

@jax.custom_vjp
def low(v):
    return lax.optimization_barrier(v.astype(jnp.bfloat16)).astype(jnp.float32)

@jax.custom_vjp
def low_back(v):
    return v

def low_keep(v):
    return (low(v), None)

def low_pass(kept, grad):
    return (grad,)

def back_keep(v):
    return (v, None)

def back_low(kept, grad):
    return (low(grad),)
low.defvjp(low_keep, low_pass)
low_back.defvjp(back_keep, back_low)

def matmul(left_side, right_side):
    return jnp.dot(left_side, right_side, precision=lax.Precision.HIGHEST, preferred_element_type=jnp.float32)

def rms_norm(vectors, gain_vec):
    return vectors * lax.rsqrt(lax.optimization_barrier(jnp.mean(vectors * vectors, axis=-1, keepdims=True)) + EPS) * gain_vec

def positions(doc_row):
    length = doc_row.shape[0]
    offsets = jnp.arange(length, dtype=jnp.int32)
    starts_here = jnp.concatenate([jnp.ones((1,), jnp.bool_), doc_row[1:] != doc_row[:-1]])
    doc_start = lax.cummax(jnp.where(starts_here, offsets, jnp.zeros_like(offsets)), axis=0)
    return offsets - doc_start

def rotary_tables(token_pos):
    half_dim = HD // 2
    frequency = THETA ** (-(jnp.arange(half_dim, dtype=jnp.float32) * 2.0) / HD)
    angles = token_pos.astype(jnp.float32)[:, None] * frequency[None, :]
    return (jnp.cos(angles)[:, None, :], jnp.sin(angles)[:, None, :])

def rotate(vectors, cosine, sine_table):
    half_dim = vectors.shape[-1] // 2
    lower_half = vectors[..., :half_dim]
    upper_half = vectors[..., half_dim:]
    return jnp.concatenate([lower_half * cosine - upper_half * sine_table, upper_half * cosine + lower_half * sine_table], axis=-1)

def attend(inputs):
    query_heads, key_heads, value_heads, doc_row = inputs
    group_size = QH // KVH
    length = query_heads.shape[0]
    offsets = jnp.arange(length, dtype=jnp.int32)
    allowed = (doc_row[:, None] == doc_row[None, :]) & (offsets[:, None] >= offsets[None, :])
    key_all = jnp.repeat(key_heads, group_size, axis=1)
    value_all = jnp.repeat(value_heads, group_size, axis=1)
    scores = jnp.einsum('qhd,khd->hqk', query_heads, key_all, precision=lax.Precision.HIGHEST) * HD ** (-0.5)
    scores = low_back(scores)
    totals = lax.optimization_barrier(jnp.sum(jnp.where(allowed[None], jnp.exp(scores), 0.0), axis=-1, keepdims=True))
    weights = jnp.where(allowed[None], jnp.exp(scores - jnp.log(totals)), 0.0)
    return jnp.einsum('hqk,khd->qhd', low(weights), value_all, precision=lax.Precision.HIGHEST)

def reference(tokens, w_query, w_key, w_value, w_out, w_gate, w_up, w_down, attn_gain, ffn_gain, query_gain, key_gain, doc_ids, out_grad):
    token_pos = jax.vmap(positions)(doc_ids).reshape(TOKENS)
    cosine, sine_table = rotary_tables(token_pos)

    def forward(token_vals, wq_vals, wk_vals, wv_vals, wo_vals, wg_vals, wu_vals, wd_vals, gain_attn, gain_ffn, gain_query, gain_key):
        normed = low(rms_norm(token_vals, gain_attn))
        query_proj = low_back(matmul(normed, wq_vals)).reshape(TOKENS, QH, HD)
        key_proj = low_back(matmul(normed, wk_vals)).reshape(TOKENS, KVH, HD)
        value_heads = low(low_back(matmul(normed, wv_vals))).reshape(N_ROW, SEQ_LEN, KVH, HD)
        query_heads = low(rotate(rms_norm(query_proj, gain_query), cosine, sine_table)).reshape(N_ROW, SEQ_LEN, QH, HD)
        key_heads = low(rotate(rms_norm(key_proj, gain_key), cosine, sine_table)).reshape(N_ROW, SEQ_LEN, KVH, HD)
        mixed_heads = lax.map(jax.checkpoint(attend), (query_heads, key_heads, value_heads, doc_ids))
        mixed_heads = low_back(low(mixed_heads.reshape(TOKENS, QH * HD)))
        hidden = token_vals + low_back(matmul(mixed_heads, wo_vals))
        ffn_input = low(rms_norm(low(hidden), gain_ffn))
        gate_proj = low_back(matmul(ffn_input, wg_vals))
        up_proj = low_back(matmul(ffn_input, wu_vals))
        inner_act = low(jax.nn.silu(gate_proj) * up_proj)
        return hidden + low_back(matmul(inner_act, wd_vals))
    result, pullback = jax.vjp(forward, tokens.astype(jnp.float32), w_query.astype(jnp.float32), w_key.astype(jnp.float32), w_value.astype(jnp.float32), w_out.astype(jnp.float32), w_gate.astype(jnp.float32), w_up.astype(jnp.float32), w_down.astype(jnp.float32), attn_gain.astype(jnp.float32), ffn_gain.astype(jnp.float32), query_gain.astype(jnp.float32), key_gain.astype(jnp.float32))
    gradients = pullback(out_grad.astype(jnp.float32))
    return (result.astype(jnp.bfloat16), gradients[0], gradients[1], gradients[2], gradients[3], gradients[4], gradients[5], gradients[6], gradients[7], gradients[8], gradients[9], gradients[10], gradients[11])
```

```python
import functools

import jax
import jax.numpy as jnp
from jax import lax
from jax.experimental import pallas as pl
from jax.experimental.pallas import tpu as pltpu
from jax.sharding import PartitionSpec as P

HD = 128
EPS = 1e-06
THETA = 1000000.0
BF = jnp.bfloat16
F32 = jnp.float32


NEAR = [(0, 1), (1, 0), (2, 3), (3, 2)]
FAR = [(0, 2), (2, 0), (1, 3), (3, 1)]


def after(value, *deps):
    return lax.optimization_barrier((value,) + deps)[0]


class Place:
    def __init__(self):
        self.rows = lax.axis_size("row")
        self.levels = self.rows // 2
        self.row = lax.axis_index("row")
        self.col = lax.axis_index("col")
        self.level = self.row // 2
        self.side = self.row % 2
        self.up = [(i, (i + 2) % self.rows) for i in range(self.rows)]
        self.across = [(i, i ^ 1) for i in range(self.rows)]
        per = self.rows // 8
        self.turn = []
        for row in range(self.rows):
            for col in range(4):
                unit, sub = divmod(row, per)
                to_row = 2 * (col * per + sub) + unit % 2
                self.turn.append((row * 4 + col, to_row * 4 + unit // 2))
        self.turn_back = [(b, a) for a, b in self.turn]

    def behind(self, steps):
        return lax.rem(self.level - steps + self.levels, self.levels)


def up(place, value):
    return lax.ppermute(value, "row", place.up)


def across(place, value):
    return lax.ppermute(value, "row", place.across)


def near(value):
    return lax.ppermute(value, "col", NEAR)


def far(value):
    return lax.ppermute(value, "col", FAR)


def ring_gather(place, shard):
    held = [shard]
    for _ in range(place.levels - 1):
        held.append(up(place, held[-1]))
    return held


def rows_gather(place, shard):
    rows = shard.shape[0]
    held = ring_gather(place, shard)
    other = [across(place, h) for h in held]
    whole = jnp.zeros((rows * place.rows, shard.shape[1]), shard.dtype)
    for steps in range(place.levels):
        base = place.behind(steps) * 2
        whole = lax.dynamic_update_slice(whole, held[steps], ((base + place.side) * rows, 0))
        whole = lax.dynamic_update_slice(whole, other[steps], ((base + 1 - place.side) * rows, 0))
    return whole, held[-2]


def ring_scatter(place, own):
    held = None
    for steps in range(1, place.levels):
        part = own(steps)
        if held is not None:
            part = (part.astype(F32) + held.astype(F32)).astype(BF)
        held = up(place, part)
    return own(0).astype(F32) + held.astype(F32)


def rows_scatter(place, term):
    rows = term.shape[0] // place.rows
    blocks = term.reshape(place.levels, 2, rows, term.shape[1])
    sent = across(place, lax.dynamic_index_in_dim(blocks, 1 - place.side, 1, False))
    kept = lax.dynamic_index_in_dim(blocks, place.side, 1, False)

    def own(steps):
        level = place.behind(steps)
        return lax.dynamic_index_in_dim(kept, level, 0, False).astype(
            F32
        ) + lax.dynamic_index_in_dim(sent, level, 0, False).astype(F32)

    return ring_scatter(place, lambda steps: own(steps).astype(BF) if steps else own(0))


def pieces_of(value):
    side = far(value)
    return (value, near(value), side, near(side))


def plane_pieces(place, value):
    half = value.shape[1] // 2
    side = far(value)
    other = across(place, value)
    diag0 = far(other[:, :half])
    diag1 = across(place, side[:, half:])
    return (
        (value, near(value), side, near(side)),
        (
            other,
            near(other),
            jnp.concatenate([diag0, diag1], axis=1),
            jnp.concatenate([near(diag0), near(diag1)], axis=1),
        ),
    )


def plane_scatter(place, send, keep):
    sent = near(send)
    rows, width = keep.shape[0] // 2, keep.shape[1] // 2
    half = width // 2

    def mine(top, lo, hi):
        at = (slice(0, rows) if top else slice(rows, None), slice(lo, hi))
        return keep[at].astype(F32) + sent[at].astype(F32)

    diag0 = far(mine(False, width, width + half).astype(BF)).astype(F32)
    diag1 = across(place, mine(False, width + half, 2 * width).astype(BF)).astype(F32)
    to_side = mine(False, 0, width) + jnp.pad(diag0, ((0, 0), (0, half)))
    to_far = mine(True, width, 2 * width) + jnp.pad(diag1, ((0, 0), (half, 0)))
    return (
        mine(True, 0, width)
        + across(place, to_side.astype(BF)).astype(F32)
        + far(to_far.astype(BF)).astype(F32)
    )


def col_scatter(send, keep):
    width = keep.shape[1] // 2
    sent = near(send)
    other = far((keep[:, width:].astype(F32) + sent[:, width:].astype(F32)).astype(BF))
    return keep[:, :width].astype(F32) + sent[:, :width].astype(F32) + other.astype(F32)


def widen_kernel(col_ref, *refs, count, norm):
    pieces, refs = refs[: 4 * count], refs[4 * count :]
    if norm:
        gain_ref, refs = refs[0], refs[1:]
    out_ref = refs[0]
    width = pieces[0].shape[1]
    group = pl.program_id(0) // (pl.num_programs(0) // count)
    for g in range(count):

        @pl.when(group == g)
        def _():
            values = [p[...] for p in pieces[4 * g : 4 * g + 4]]
            if norm:
                values = [v.astype(F32) for v in values]
                total = sum(jnp.sum(v * v, axis=1, keepdims=True) for v in values)
                scale = lax.rsqrt(total / (4 * width) + EPS)
                refs[1][...] = scale
            for flip, v in enumerate(values):
                at = pl.ds(pl.multiple_of((col_ref[0] ^ flip) * width, width), width)
                if norm:
                    v = (v * scale * gain_ref[:, at]).astype(BF)
                out_ref[:, at] = v


def widen(place, groups, gain=None, tile=256):
    count = len(groups)
    length, width = groups[0][0].shape
    steps = length // tile

    def piece_map(g):
        return lambda i, col: (jnp.clip(i - g * steps, 0, steps - 1), 0)

    in_specs = [pl.BlockSpec((tile, width), piece_map(g)) for g in range(count) for _ in range(4)]
    args = [p for group in groups for p in group]
    out_shape = [jax.ShapeDtypeStruct((count * length, 4 * width), BF)]
    out_specs = [pl.BlockSpec((tile, 4 * width), lambda i, col: (i, 0))]
    if gain is not None:
        in_specs.append(pl.BlockSpec((1, 4 * width), lambda i, col: (0, 0)))
        args.append(gain[None])
        out_shape.append(jax.ShapeDtypeStruct((count * length, 1), F32))
        out_specs.append(pl.BlockSpec((tile, 1), lambda i, col: (i, 0)))
    out = pl.pallas_call(
        functools.partial(widen_kernel, count=count, norm=gain is not None),
        grid_spec=pltpu.PrefetchScalarGridSpec(
            num_scalar_prefetch=1,
            grid=(count * steps,),
            in_specs=in_specs,
            out_specs=out_specs,
        ),
        out_shape=out_shape,
        cost_estimate=pl.CostEstimate(
            flops=10 * count * length * width * 4,
            bytes_accessed=16 * count * length * width,
            transcendentals=0,
        ),
        name="widen",
    )(place.col.reshape(1), *args)
    return out if gain is not None else out[0]


def back_kernel(order_ref, grads_ref, weight_ref, send_ref, keep_ref):
    part = lax.dot_general(
        grads_ref[...], weight_ref[...], (((1,), (1,)), ((), ())), preferred_element_type=F32
    ).astype(BF)
    step = pl.program_id(0)

    @pl.when(step < 2)
    def _():
        send_ref[...] = part

    @pl.when(step >= 2)
    def _():
        keep_ref[...] = part


def back_blocks(place, grads_in, weight):
    length, depth = grads_in.shape
    width = weight.shape[0] // 4
    order = place.col ^ jnp.array([1, 3, 0, 2], jnp.int32)
    return pl.pallas_call(
        back_kernel,
        grid_spec=pltpu.PrefetchScalarGridSpec(
            num_scalar_prefetch=1,
            grid=(4,),
            in_specs=[
                pl.BlockSpec((length, depth), lambda j, order: (0, 0)),
                pl.BlockSpec((width, depth), lambda j, order: (order[j], 0)),
            ],
            out_specs=[
                pl.BlockSpec((length, width), lambda j, order: (0, jnp.minimum(j, 1))),
                pl.BlockSpec((length, width), lambda j, order: (0, jnp.maximum(j - 2, 0))),
            ],
        ),
        out_shape=[jax.ShapeDtypeStruct((length, 2 * width), BF)] * 2,
        cost_estimate=pl.CostEstimate(
            flops=8 * length * depth * width,
            bytes_accessed=2 * (length * depth + 4 * width * depth + 4 * length * width),
            transcendentals=0,
        ),
        name="back_blocks",
    )(order, grads_in, weight)


def ffn_kernel(
    col_ref, x_ref, og_ref, gate_ref, up_ref, down_ref,
    inner_ref, gg_ref, ug_ref, send_ref, keep_ref, rsend_ref, rkeep_ref,
):
    nt = (((1,), (1,)), ((), ()))
    x = x_ref[...]
    gate = jnp.dot(x, gate_ref[...], preferred_element_type=F32)
    up_val = jnp.dot(x, up_ref[...], preferred_element_type=F32)
    in_g = lax.dot_general(og_ref[...], down_ref[...], nt, preferred_element_type=F32)
    sig = jax.nn.sigmoid(gate)
    act = gate * sig
    inner = (act * up_val).astype(BF)
    gate_g = (in_g * up_val * sig * (1.0 + gate * (1.0 - sig))).astype(BF)
    up_g = (in_g * act).astype(BF)
    inner_ref[...] = inner
    gg_ref[...] = gate_g
    ug_ref[...] = up_g
    width = gate_ref.shape[0] // 4
    for slot, flip in enumerate((1, 3, 0, 2)):
        at = pl.ds(pl.multiple_of((col_ref[0] ^ flip) * width, width), width)
        to = slice((slot % 2) * width, (slot % 2 + 1) * width)
        part = lax.dot_general(gate_g, gate_ref[at, :], nt, preferred_element_type=F32)
        part += lax.dot_general(up_g, up_ref[at, :], nt, preferred_element_type=F32)
        (send_ref if slot < 2 else keep_ref)[:, to] = part.astype(BF)
        res = jnp.dot(inner, down_ref[:, at], preferred_element_type=F32)
        (rsend_ref if slot < 2 else rkeep_ref)[:, to] = res.astype(BF)


def ffn(place, ffn_input, wide_grad, gate, up_weight, down, tile=512):
    length, full = ffn_input.shape
    units = gate.shape[1]

    def rows(n):
        return pl.BlockSpec((tile, n), lambda i, col: (i, 0))

    def whole(w):
        return pl.BlockSpec(w.shape, lambda i, col: (0, 0), pipeline_mode=pl.Buffered(1))

    return pl.pallas_call(
        ffn_kernel,
        grid_spec=pltpu.PrefetchScalarGridSpec(
            num_scalar_prefetch=1,
            grid=(length // tile,),
            in_specs=[rows(full), rows(full), whole(gate), whole(up_weight), whole(down)],
            out_specs=[rows(units)] * 3 + [rows(full // 2)] * 4,
        ),
        out_shape=[jax.ShapeDtypeStruct((length, units), BF)] * 3
        + [jax.ShapeDtypeStruct((length, full // 2), BF)] * 4,
        cost_estimate=pl.CostEstimate(
            flops=12 * length * full * units,
            bytes_accessed=8 * length * full + 6 * length * units + 6 * full * units,
            transcendentals=length * units,
        ),
        name="ffn",
    )(place.col.reshape(1), ffn_input, wide_grad, gate, up_weight, down)


def col_sum(value):
    value = value + near(value)
    return value + far(value)


def dot_f32(left, right):
    return jnp.dot(left, right, preferred_element_type=F32)


def weight_term(left_side, grads_in):
    return lax.dot_general(
        left_side, grads_in, (((0,), (0,)), ((), ())), preferred_element_type=F32
    ).astype(BF)


def norm_back(summed, inputs_local, gain_vec, scale_rows):
    full_width = gain_vec.shape[0]
    share_cols = inputs_local.shape[1]
    col_start = lax.axis_index("col") * share_cols
    local_in = inputs_local.astype(F32)
    local_gain = lax.dynamic_slice_in_dim(gain_vec, col_start, share_cols, 0)
    row_stat = col_sum(jnp.sum(local_gain * summed * local_in, axis=1, keepdims=True))
    grad_local = scale_rows * local_gain * summed - local_in * scale_rows**3 * row_stat / full_width
    gain_part = jnp.sum(summed * local_in * scale_rows, axis=0)
    return (grad_local, gain_part)


def rotary_tables(doc_row):
    length = doc_row.shape[0]
    offsets = jnp.arange(length, dtype=jnp.int32)
    starts_here = jnp.concatenate([jnp.ones((1,), jnp.bool_), doc_row[1:] != doc_row[:-1]])
    doc_start = lax.cummax(jnp.where(starts_here, offsets, jnp.zeros_like(offsets)), axis=0)
    half_dim = HD // 2
    frequency = THETA ** (-(jnp.arange(half_dim, dtype=F32) * 2.0) / HD)
    angles = (offsets - doc_start).astype(F32)[:, None] * frequency[None, :]
    cosine, sine = jnp.cos(angles), jnp.sin(angles)
    return (
        jnp.concatenate([cosine, cosine], axis=1),
        jnp.concatenate([-sine, sine], axis=1),
        doc_start[:, None],
    )


NT = (((1,), (1,)), ((), ()))
TN = (((0,), (0,)), ((), ()))


def swap(value):
    return pltpu.roll(value, HD // 2, 1)


def head(value, h):
    return value[:, h * HD : (h + 1) * HD]


def window_probs(step, tile, query, keys, start):
    base = jnp.maximum(step - 2, 0) * tile
    scores = lax.dot_general(query, keys, NT, preferred_element_type=F32) * HD ** (-0.5)
    key_at = base + lax.broadcasted_iota(jnp.int32, scores.shape, 1)
    row = lax.broadcasted_iota(jnp.int32, scores.shape, 0)
    query_at = step * tile + jnp.where(row >= tile, row - tile, row)
    allowed = (key_at >= start) & (key_at <= query_at)
    exps = jnp.where(allowed, jnp.exp(scores), 0.0)
    return exps, 1.0 / jnp.sum(exps, axis=1, keepdims=True)


def attend_kernel(
    col_ref, *refs, heads, groups
):
    pieces, refs = refs[:4], refs[4:]
    gain_ref, w_ref, hgain_ref, cos_ref, sin_ref, start_ref = refs[:6]
    x_ref, scale_ref, q_ref, k_ref, v_ref, raw_ref, mixed_ref, k_all, v_all = refs[6:]
    step = pl.program_id(0)
    tile, width = pieces[0].shape
    values = [p[...].astype(F32) for p in pieces]
    total = sum(jnp.sum(v * v, axis=1, keepdims=True) for v in values)
    scale = lax.rsqrt(total / (4 * width) + EPS)
    scale_ref[...] = scale
    for flip, v in enumerate(values):
        at = pl.ds(pl.multiple_of((col_ref[0] ^ flip) * width, width), width)
        x_ref[:, at] = (v * scale * gain_ref[:, at]).astype(BF)
    raw = jnp.dot(x_ref[...], w_ref[...], preferred_element_type=F32)
    raw_ref[...] = raw[:, : (heads + groups) * HD].astype(BF)
    cosine, sine = cos_ref[...], sin_ref[...]

    @pl.when(step == 0)
    def _():
        k_all[...] = jnp.zeros_like(k_all)
        v_all[...] = jnp.zeros_like(v_all)

    rows = pl.ds(pl.multiple_of(step * tile, tile), tile)
    queries = []
    for h in range(heads + groups):
        u = head(raw, h)
        gain = hgain_ref[0:1] if h < heads else hgain_ref[1:2]
        n = u * lax.rsqrt(jnp.mean(u * u, axis=1, keepdims=True) + EPS) * gain
        r = (n * cosine + swap(n) * sine).astype(BF)
        if h < heads:
            q_ref[:, h * HD : (h + 1) * HD] = r
            queries.append(r)
        else:
            k_all[rows, (h - heads) * HD : (h - heads + 1) * HD] = r
    v_all[rows, :] = raw[:, (heads + groups) * HD :].astype(BF)
    k_ref[...] = k_all[rows, :]
    v_ref[...] = v_all[rows, :]
    window = pl.ds(pl.multiple_of(jnp.maximum(step - 2, 0) * tile, tile), 3 * tile)
    per = heads // groups
    start = jnp.concatenate([start_ref[...]] * 2, axis=0)
    for g in range(groups):
        for pair in range(0, per, 2):
            h = g * per + pair
            exps, inverse = window_probs(
                step, tile, jnp.concatenate(queries[h : h + 2], axis=0),
                k_all[window, g * HD : (g + 1) * HD], start,
            )
            mixed = jnp.dot(
                (exps * inverse).astype(BF),
                v_all[window, g * HD : (g + 1) * HD],
                preferred_element_type=F32,
            ).astype(BF)
            mixed_ref[:, h * HD : (h + 1) * HD] = mixed[:tile]
            mixed_ref[:, (h + 1) * HD : (h + 2) * HD] = mixed[tile:]


def attend(place, pieces, gain, weight, head_gains, tables, heads, groups, tile=256):
    length, width = pieces[0].shape
    cosine, sine, start = tables

    def rows(n):
        return pl.BlockSpec((tile, n), lambda i, col: (i, 0))

    def whole(w):
        return pl.BlockSpec(w.shape, lambda i, col: (0, 0), pipeline_mode=pl.Buffered(1))

    sizes = [
        (4 * width, BF), (1, F32), (heads * HD, BF), (groups * HD, BF), (groups * HD, BF),
        ((heads + groups) * HD, BF), (heads * HD, BF),
    ]
    return pl.pallas_call(
        functools.partial(attend_kernel, heads=heads, groups=groups),
        grid_spec=pltpu.PrefetchScalarGridSpec(
            num_scalar_prefetch=1,
            grid=(length // tile,),
            in_specs=[rows(width)] * 4
            + [whole(gain), whole(weight), whole(head_gains), rows(HD), rows(HD), rows(1)],
            out_specs=[rows(n) for n, _ in sizes],
            scratch_shapes=[pltpu.VMEM((length, groups * HD), BF)] * 2,
        ),
        out_shape=[jax.ShapeDtypeStruct((length, n), t) for n, t in sizes],
        cost_estimate=pl.CostEstimate(
            flops=2 * length * weight.size + 12 * length * tile * heads * HD,
            bytes_accessed=2 * weight.size + 20 * length * width,
            transcendentals=3 * length * tile * heads,
        ),
        name="attend",
    )(place.col.reshape(1), *pieces, gain, weight, head_gains, cosine, sine, start)


def head_back(grad, raw, gain, cosine, sine):
    e = grad * cosine - swap(grad) * sine
    s = lax.rsqrt(jnp.mean(raw * raw, axis=1, keepdims=True) + EPS)
    er = e * raw
    stat = jnp.sum(gain * er, axis=1, keepdims=True)
    return s * gain * e - raw * (s * s * s * stat / HD), jnp.sum(er * s, axis=0, keepdims=True)


def attend_back_kernel(
    q_ref, k_ref, v_ref, do_ref, raw_ref, hgain_ref, cos_ref, sin_ref, start_ref,
    g_ref, gains_ref, dk, dv, *, heads, groups,
):
    step = pl.program_id(0)
    tile = q_ref.shape[0]
    low = HD ** (-0.5)

    @pl.when(step == 0)
    def _():
        dk[...] = jnp.zeros_like(dk)
        dv[...] = jnp.zeros_like(dv)
        gains_ref[...] = jnp.zeros_like(gains_ref)

    rows = pl.ds(pl.multiple_of(step * tile, tile), tile)
    window = pl.ds(pl.multiple_of(jnp.maximum(step - 2, 0) * tile, tile), 3 * tile)
    per = heads // groups
    start = jnp.concatenate([start_ref[...]] * 2, axis=0)
    cosine, sine = cos_ref[rows, :], sin_ref[rows, :]
    for g in range(groups):
        lanes = slice(g * HD, (g + 1) * HD)
        keys, values = k_ref[window, lanes], v_ref[window, lanes]
        for pair in range(0, per, 2):
            h = g * per + pair
            query = jnp.concatenate([head(q_ref, h), head(q_ref, h + 1)], axis=0)
            grad = jnp.concatenate([head(do_ref, h), head(do_ref, h + 1)], axis=0)
            exps, inverse = window_probs(step, tile, query, keys, start)
            probs = exps * inverse
            dp = lax.dot_general(grad, values, NT, preferred_element_type=F32)
            row_dot = jnp.sum(probs * dp, axis=1, keepdims=True)
            ds = (probs * (dp - row_dot)).astype(BF)
            dq = jnp.dot(ds, keys, preferred_element_type=F32) * low
            dk[window, lanes] += lax.dot_general(ds, query, TN, preferred_element_type=F32) * low
            dv[window, lanes] += lax.dot_general(
                probs.astype(BF), grad, TN, preferred_element_type=F32
            )
            for k in range(2):
                at = slice((h + k) * HD, (h + k + 1) * HD)
                out, term = head_back(
                    dq[k * tile : (k + 1) * tile],
                    raw_ref[rows, at].astype(F32),
                    hgain_ref[0:1],
                    cosine,
                    sine,
                )
                g_ref[rows, at] = out.astype(BF)
                gains_ref[0:1] += term

    @pl.when(step == pl.num_programs(0) - 1)
    def _():
        g_ref[:, (heads + groups) * HD :] = dv[...].astype(BF)
        for g in range(groups):
            at = slice((heads + g) * HD, (heads + g + 1) * HD)
            out, term = head_back(
                dk[:, g * HD : (g + 1) * HD],
                raw_ref[:, at].astype(F32),
                hgain_ref[1:2],
                cos_ref[...],
                sin_ref[...],
            )
            g_ref[:, at] = out.astype(BF)
            gains_ref[1:2] += term


def attend_back(queries, keys, values, mixed_grads, raw, head_gains, tables, tile=256):
    length = queries.shape[0]
    heads, groups = queries.shape[1] // HD, keys.shape[1] // HD
    cosine, sine, start = tables

    def rows(n):
        return pl.BlockSpec((tile, n), lambda i: (i, 0))

    def whole(w):
        return pl.BlockSpec(w.shape, lambda i: (0, 0), pipeline_mode=pl.Buffered(1))

    wide = (heads + 2 * groups) * HD
    return pl.pallas_call(
        functools.partial(attend_back_kernel, heads=heads, groups=groups),
        grid_spec=pl.GridSpec(
            grid=(length // tile,),
            in_specs=[
                rows(heads * HD), whole(keys), whole(values), rows(heads * HD), whole(raw),
                whole(head_gains), whole(cosine), whole(sine), rows(1),
            ],
            out_specs=[
                pl.BlockSpec((length, wide), lambda i: (0, 0)),
                pl.BlockSpec((2, HD), lambda i: (0, 0)),
            ],
            scratch_shapes=[pltpu.VMEM((length, groups * HD), F32)] * 2,
        ),
        out_shape=[
            jax.ShapeDtypeStruct((length, wide), BF),
            jax.ShapeDtypeStruct((2, HD), F32),
        ],
        cost_estimate=pl.CostEstimate(
            flops=30 * length * tile * heads * HD,
            bytes_accessed=12 * length * heads * HD,
            transcendentals=3 * length * tile * heads,
        ),
        name="attend_back",
    )(queries, keys, values, mixed_grads, raw, head_gains, cosine, sine, start)


def mix_kernel(col_ref, *refs):
    pieces, (w_ref, tok_ref, wide_ref, hidden_ref, low_ref) = refs[:4], refs[4:]
    width = pieces[0].shape[1]
    total = tok_ref[...].astype(F32)
    for flip, p in enumerate(pieces):
        at = pl.ds(pl.multiple_of((col_ref[0] ^ flip) * width, width), width)
        value = p[...]
        wide_ref[:, at] = value
        total += jnp.dot(value, w_ref[at, :], preferred_element_type=F32)
    hidden_ref[...] = total
    low_ref[...] = total.astype(BF)


def mix(place, pieces, weight, tokens, tile=512):
    length, width = pieces[0].shape
    share = tokens.shape[1]

    def rows(n):
        return pl.BlockSpec((tile, n), lambda i, col: (i, 0))

    return pl.pallas_call(
        mix_kernel,
        grid_spec=pltpu.PrefetchScalarGridSpec(
            num_scalar_prefetch=1,
            grid=(length // tile,),
            in_specs=[rows(width)] * 4
            + [
                pl.BlockSpec(weight.shape, lambda i, col: (0, 0), pipeline_mode=pl.Buffered(1)),
                rows(share),
            ],
            out_specs=[rows(4 * width), rows(share), rows(share)],
        ),
        out_shape=[
            jax.ShapeDtypeStruct((length, 4 * width), BF),
            jax.ShapeDtypeStruct((length, share), F32),
            jax.ShapeDtypeStruct((length, share), BF),
        ],
        cost_estimate=pl.CostEstimate(
            flops=2 * length * weight.size,
            bytes_accessed=2 * weight.size + 24 * length * width,
            transcendentals=0,
        ),
        name="mix",
    )(place.col.reshape(1), *pieces, weight, tokens)


def row_sum(place, value):
    value = value + across(place, value)
    hop = 2
    while hop < place.rows:
        value = value + lax.ppermute(value, "row", [(i, i ^ hop) for i in range(place.rows)])
        hop *= 2
    return value


def side_halves(place, weight):
    rows, cols = weight.shape
    half = cols // 2
    other = across(
        place, lax.dynamic_slice_in_dim(weight, (1 - place.side) * half, half, 1)
    )
    mine = lax.dynamic_slice_in_dim(weight, place.side * half, half, 1)
    both = lax.dynamic_update_slice(
        jnp.zeros((2 * rows, half), weight.dtype), mine, (place.side * rows, 0)
    )
    return lax.dynamic_update_slice(both, other, ((1 - place.side) * rows, 0))


def side_gather(place, both):
    rows = both.shape[0]
    whole = jnp.zeros((rows * place.levels, both.shape[1]), both.dtype)
    held = ring_gather(place, both)
    for steps, piece in enumerate(held):
        whole = lax.dynamic_update_slice(whole, piece, (place.behind(steps) * rows, 0))
    return whole, held[-2]


def side_scatter(place, term):
    rows = term.shape[0] // place.levels
    half = term.shape[1]
    both = ring_scatter(
        place, lambda steps: lax.dynamic_slice_in_dim(term, place.behind(steps) * rows, rows, 0)
    )
    rows //= 2
    mine = lax.dynamic_slice_in_dim(both, place.side * rows, rows, 0)
    other = across(
        place, lax.dynamic_slice_in_dim(both, (1 - place.side) * rows, rows, 0).astype(BF)
    )
    out = lax.dynamic_update_slice(
        jnp.zeros((rows, 2 * half), F32), mine, (0, place.side * half)
    )
    return lax.dynamic_update_slice(out, other.astype(F32), (0, (1 - place.side) * half))


def down_block(place, steps):
    per = place.rows // 8
    level = place.behind(steps)
    return level % per, level // per


def down_gather(place, turned):
    per = place.rows // 8
    rows, cols = turned.shape
    whole = jnp.zeros((per * rows, 4 * cols), turned.dtype)
    held = ring_gather(place, turned)
    for steps, piece in enumerate(held):
        i, j = down_block(place, steps)
        whole = lax.dynamic_update_slice(whole, piece, (i * rows, j * cols))
    return whole, held[-2]


def down_scatter(place, term):
    per = place.rows // 8
    rows, cols = term.shape[0] // per, term.shape[1] // 4

    def own(steps):
        i, j = down_block(place, steps)
        return lax.dynamic_slice(term, (i * rows, j * cols), (rows, cols))

    summed = ring_scatter(place, own).astype(BF)
    return lax.ppermute(summed, ("row", "col"), place.turn_back).astype(F32)


def body(
    tokens,
    w_query,
    w_key,
    w_value,
    w_out,
    w_gate,
    w_up,
    w_down,
    attn_gain,
    ffn_gain,
    query_gain,
    key_gain,
    doc_ids,
    out_grad,
):
    place = Place()
    length, share = tokens.shape
    tables = rotary_tables(doc_ids[0])
    head_gains = jnp.stack([query_gain, key_gain])
    query_cols = w_query.shape[1]
    key_cols = w_key.shape[1]

    w_qkv, token = rows_gather(place, jnp.concatenate([w_query, w_key, w_value], axis=1))
    token_pieces = pieces_of(tokens)
    own_down = after(lax.ppermute(w_down, ("row", "col"), place.turn), token)
    own_gate = after(side_halves(place, w_gate), token)
    own_up = after(side_halves(place, w_up), token)
    w_mix, token = rows_gather(place, after(w_out, token))
    down, token = down_gather(place, after(own_down, token))
    gate, token1 = side_gather(place, after(own_gate, token))
    up_weight, token = side_gather(place, after(own_up, token1))

    heads, groups = query_cols // HD, key_cols // HD
    attn_input, attn_scale, queries, keys, values, raw, mixed = attend(
        place, token_pieces, attn_gain[None], w_qkv, head_gains, tables, heads, groups
    )
    wide_mixed, hidden, hidden_low = mix(place, pieces_of(mixed), w_mix, tokens)

    wide_grad = widen(place, plane_pieces(place, out_grad))
    ffn_input, scales = widen(place, plane_pieces(place, hidden_low), ffn_gain)
    ffn_scale = scales[:length]
    inner, gate_g, up_g, send, keep, res_send, res_keep = ffn(
        place, ffn_input, wide_grad, gate, up_weight, down
    )
    summed = plane_scatter(place, send, keep)
    gate_wg = side_scatter(place, weight_term(ffn_input, gate_g))
    up_wg = side_scatter(place, weight_term(ffn_input, up_g))
    down_wg = down_scatter(place, weight_term(inner, wide_grad))
    result = (hidden + plane_scatter(place, res_send, res_keep)).astype(BF)
    hidden_part, ffn_gain_term = norm_back(summed, hidden_low, ffn_gain, ffn_scale)
    hidden_grads = out_grad.astype(F32) + hidden_part

    branch_grads = hidden_grads.astype(BF)
    mixed_grads = col_scatter(*back_blocks(place, branch_grads, w_mix)).astype(BF)
    out_wg = rows_scatter(place, weight_term(wide_mixed, branch_grads))
    qkv_grads, heads_term = attend_back(
        queries, keys, values, mixed_grads, raw, head_gains, tables
    )
    qkv_wg = rows_scatter(place, weight_term(attn_input, qkv_grads))
    attn_sum = col_scatter(*back_blocks(place, qkv_grads, w_qkv))
    token_part, attn_gain_term = norm_back(attn_sum, tokens, attn_gain, attn_scale)
    token_grads = hidden_grads + token_part

    wide = row_sum(place, jnp.stack([attn_gain_term, ffn_gain_term]))
    gains = lax.dynamic_update_slice(jnp.zeros((2, 4 * share), F32), wide, (0, place.col * share))
    gains = col_sum(gains)
    heads = col_sum(row_sum(place, heads_term))
    return (
        result,
        token_grads,
        qkv_wg[:, :query_cols],
        qkv_wg[:, query_cols : query_cols + key_cols],
        qkv_wg[:, query_cols + key_cols :],
        out_wg,
        gate_wg,
        up_wg,
        down_wg,
        gains[0],
        gains[1],
        heads[0],
        heads[1],
    )


def solution(mesh):
    return jax.shard_map(
        body,
        mesh=mesh,
        in_specs=(
            P("row", "col"),
            P("row", "col"),
            P("row", "col"),
            P("row", "col"),
            P("row", "col"),
            P("row", "col"),
            P("row", "col"),
            P("row", "col"),
            P(),
            P(),
            P(),
            P(),
            P("row", None),
            P("row", "col"),
        ),
        out_specs=(
            P("row", "col"),
            P("row", "col"),
            P("row", "col"),
            P("row", "col"),
            P("row", "col"),
            P("row", "col"),
            P("row", "col"),
            P("row", "col"),
            P("row", "col"),
            P(),
            P(),
            P(),
            P(),
        ),
        check_vma=False,
    )
```
